32 devices in a mesh: dp: 4 (over y, x), seq: 4 (over z), tensor: 2 (over core).
Axes of the slice: x: 2, y: 2, z: 4, core: 2. Of those that a mesh axis runs over, the one named last changes fastest.
Arguments:
- queries: bfloat16 [4, 256, 8192], P('dp', 'seq', 'tensor'), may hold values from -6 to 6
- new_keys: bfloat16 [4, 256, 1024], P('dp', 'seq', 'tensor'), may hold values from -6 to 6
- new_values: bfloat16 [4, 256, 1024], P('dp', 'seq', 'tensor'), may hold values from -6 to 6
- cache_keys: bfloat16 [4, 2048, 1024], P('dp', 'seq', 'tensor'), may hold values from -6 to 6
- cache_values: bfloat16 [4, 2048, 1024], P('dp', 'seq', 'tensor'), may hold values from -6 to 6
- keep_lengths: int32 [4, 4], P('dp', 'seq'), may hold values from 1 to 512
- cache_doc: int32 [4, 2048], P('dp', 'seq'), may hold values from 0 to 1
- new_doc: int32 [4, 256], P('dp', 'seq'), may hold values from 0 to 1, never falling along the last dimension, each value on 1 to 160 neighbouring positions
- out_weight: bfloat16 [8192, 8192], P('tensor', 'dp'), may hold values from -0.0625 to 0.0625
Outputs:
- mixed_out: bfloat16 [4, 256, 4, 2048], P('dp', 'seq', None, 'tensor')
The draws below stay inside these ranges and needn't reach their ends.
Inputs may be any that keep to these rules, and one draw needn't show every extreme that they name: `keep_lengths`: valid cache rows of a shard come first. `cache_doc`: documents 0 and 1 of the pack. `new_doc`: never falling along the tokens of a pack; both documents present.
All inputs are finite; a program needn't handle non-finite values.
Results may differ from the reference program's by a relative error of at most 0.0056.
Values may be sent and summed in bfloat16 or wider, within the bound.
A program may use at most 128 MiB of HBM per device.

```python
import math
import jax
import jax.numpy as jnp
import numpy as np
from jax import lax

D = 8192
HQ = 64
KVH = 8
HD = 128
CACHE_DEV = 512
GROUP = 8
NEW = 256
PACKS = 4
SHARDS = 4
BLOCKS = 4
COLS = 2048


def base_values(key, width):
    result = jnp.clip(jax.random.normal(key, (PACKS, NEW, width), jnp.float32), -6.0, 6.0)
    return result


def draw_queries(key, part):
    result = base_values(jax.random.fold_in(key, 11), HQ * HD).reshape(PACKS, NEW, HQ, HD)
    return result.reshape(PACKS, NEW, HQ * HD).astype(jnp.bfloat16)


def draw_new_keys(key, part):
    result = base_values(jax.random.fold_in(key, 13), KVH * HD).reshape(PACKS, NEW, KVH, HD)
    return result.reshape(PACKS, NEW, KVH * HD).astype(jnp.bfloat16)


def with_ends(values, rng, least, top_value):
    spot = [jax.random.randint(jax.random.fold_in(rng, axis), (), 0, length) for axis, length in enumerate(values.shape)]
    longest = values.shape.index(max(values.shape))
    neighbour = spot[:longest] + [(spot[longest] + 1) % values.shape[longest]] + spot[longest + 1:]
    return values.at[tuple(spot)].set(least).at[tuple(neighbour)].set(top_value)


def levels(rng, shape, pieces, least, top_value):
    def one(dim, parts):
        heights = jax.random.uniform(jax.random.fold_in(jax.random.fold_in(rng, 6), dim), (parts,), jnp.float32, least / len(pieces), top_value / len(pieces))
        return jnp.repeat(jnp.exp(heights), shape[dim] // parts).reshape((-1,) + (1,) * (len(shape) - dim - 1))

    factor_of = one(*pieces[0])
    for cut in pieces[1:]:
        factor_of = factor_of * one(*cut)
    return factor_of


def profile(count, total, reach, skew):
    weights = [(1 << 20) // math.isqrt(rank ** skew) + 1 for rank in range(2, count + 1)]
    surplus, counts = total - reach - (count - 1), [1] * (count - 1)
    while surplus > 0:
        candidates = [i for i in range(count - 1) if counts[i] < reach]
        pool, remaining = sum([weights[i] for i in candidates]), surplus
        for i in candidates:
            more = min(reach - counts[i], max(1, remaining * weights[i] // pool), surplus)
            counts[i] = counts[i] + more
            surplus = surplus - more
    return np.array([reach] + counts)


def ragged_sizes(own_key, amount, total, reach, lean):
    if amount == 2:
        one = jax.random.randint(own_key, (), max(1, total - reach), min(reach, total - 1) + 1)
        return jnp.stack([one, total - one])
    sizes = jnp.asarray(profile(amount, total, reach, lean), jnp.int32)
    twos = (amount - 1) // 2
    giver, receiver = sizes[1:1 + 2 * twos:2], sizes[2:2 + 2 * twos:2]
    margin = jnp.minimum(giver - 1, reach - receiver)
    shifted = jax.random.randint(jax.random.fold_in(own_key, 1), (twos,), 0, 1 << 20) % (margin + 1)
    sizes = sizes.at[1:1 + 2 * twos:2].set(giver - shifted).at[2:2 + 2 * twos:2].set(receiver + shifted)
    return sizes[jax.random.permutation(jax.random.fold_in(own_key, 2), amount)]


def bell_draw(rng, extent, spread, most, pieces=(), held_as=jnp.bfloat16):
    entries = spread * jax.random.normal(rng, extent, jnp.float32)
    if pieces:
        entries = entries * levels(rng, extent, pieces, -0.22, 0.18)
    return jnp.clip(entries, -most, most).astype(held_as)


def setup_inputs(seed: int = 0) -> dict:
    key_of = jax.random.split(jax.random.key(seed), 10)
    queries = draw_queries(jax.random.fold_in(key_of[9], 71), 0)
    new_keys = draw_new_keys(jax.random.fold_in(key_of[9], 71), 0)
    new_values = bell_draw(key_of[2], (PACKS, NEW, KVH * HD), 1.0, 6.0, ((0, 4), (1, 4), (2, 2)))
    cache_keys = bell_draw(key_of[3], (PACKS, SHARDS * CACHE_DEV, KVH * HD), 1.0, 6.0, ((0, 4), (1, 4), (2, 2)))
    cache_values = bell_draw(key_of[4], (PACKS, SHARDS * CACHE_DEV, KVH * HD), 1.0, 6.0, ((0, 4), (1, 4), (2, 2)))
    keep_lengths = with_ends(jax.random.randint(key_of[5], (PACKS, SHARDS), 1, CACHE_DEV + 1), jax.random.fold_in(key_of[5], 1), 1, CACHE_DEV).astype(jnp.int32)
    cache_doc = with_ends(jax.random.randint(key_of[6], (PACKS, SHARDS * CACHE_DEV), 0, 2), jax.random.fold_in(key_of[6], 1), 0, 1).astype(jnp.int32)
    new_doc = jax.vmap(lambda own: jnp.searchsorted(jnp.cumsum(ragged_sizes(own, 2, NEW, NEW * 5 // 8, 0)), jnp.arange(NEW), side="right"))(jax.random.split(key_of[7], PACKS)).reshape((PACKS, NEW)).astype(jnp.int32)
    out_weight = bell_draw(key_of[8], (HQ * HD, D), (HQ * HD) ** -0.5, 0.0625, ((0, 2), (1, 4)))
    return {"queries": queries, "new_keys": new_keys, "new_values": new_values, "cache_keys": cache_keys, "cache_values": cache_values, "keep_lengths": keep_lengths, "cache_doc": cache_doc, "new_doc": new_doc, "out_weight": out_weight}


masked_score = -1.0e30


def softmax_terms(scores, visible, value_rows):
    scores = jnp.where(visible, scores, masked_score)
    top_score = jnp.max(scores, axis=-1)
    weights = jnp.where(visible, jnp.exp(scores - top_score[..., None]), 0.0)
    weight_sum = jnp.sum(weights, axis=-1)
    summed = jnp.dot(weights.astype(jnp.bfloat16), value_rows, preferred_element_type=jnp.float32)
    return top_score, weight_sum, summed


def reference(queries, new_keys, new_values, cache_keys, cache_values, keep_lengths, cache_doc, new_doc, out_weight):
    score_scale = HD ** -0.5
    row_token = jnp.arange(NEW * GROUP, dtype=jnp.int32) // GROUP
    positions = jnp.arange(CACHE_DEV, dtype=jnp.int32)
    new_index = jnp.arange(NEW, dtype=jnp.int32)
    outputs = []
    for pack_index in range(PACKS):
        query_heads = queries[pack_index].reshape(NEW, KVH, GROUP, HD).transpose(1, 0, 2, 3)
        cache_k = cache_keys[pack_index].reshape(SHARDS, CACHE_DEV, KVH, HD).transpose(2, 0, 1, 3)
        cache_v = cache_values[pack_index].reshape(SHARDS, CACHE_DEV, KVH, HD).transpose(2, 0, 1, 3)
        fresh_k = new_keys[pack_index].reshape(NEW, KVH, HD).transpose(1, 0, 2)
        fresh_v = new_values[pack_index].reshape(NEW, KVH, HD).transpose(1, 0, 2)
        token_doc = new_doc[pack_index]
        row_doc = jnp.repeat(token_doc, GROUP)
        shard_doc = cache_doc[pack_index].reshape(SHARDS, CACHE_DEV)
        lengths = keep_lengths[pack_index]

        def one_head(inputs):
            query_part, key_part, value_part, fresh_keys, fresh_values = inputs
            query_rows = query_part.reshape(NEW * GROUP, HD)

            def one_shard(shard_data):
                key_rows, value_rows, doc_rows, length = shard_data
                scores = jnp.dot(query_rows, key_rows.T, preferred_element_type=jnp.float32) * score_scale
                visible = (positions[None, :] < length) & (doc_rows[None, :] == row_doc[:, None])
                return softmax_terms(scores, visible, value_rows)

            shard_tops, shard_sums, shard_partial = lax.map(one_shard, (key_part, value_part, shard_doc, lengths))
            scores = jnp.dot(query_rows, fresh_keys.T, preferred_element_type=jnp.float32) * score_scale
            visible = (new_index[None, :] <= row_token[:, None]) & (token_doc[None, :] == row_doc[:, None])
            fresh_top, fresh_sum, fresh_partial = softmax_terms(scores, visible, fresh_values)
            all_tops = jnp.concatenate([shard_tops, fresh_top[None]], 0)
            overall_top = jnp.max(all_tops, axis=0)
            factors = jnp.exp(all_tops - overall_top[None])
            denominator = jnp.sum(shard_sums * factors[:-1], 0) + fresh_sum * factors[-1]
            numerator = jnp.sum(shard_partial * factors[:-1, :, None], 0) + fresh_partial * factors[-1][:, None]
            return (numerator / denominator[:, None]).reshape(NEW, GROUP, HD)

        heads_out = lax.map(one_head, (query_heads, cache_k, cache_v, fresh_k, fresh_v))
        attended = heads_out.transpose(1, 0, 2, 3).reshape(NEW, HQ * HD).astype(jnp.bfloat16)
        mixed_out = jnp.dot(attended, out_weight, preferred_element_type=jnp.float32).astype(jnp.bfloat16)
        outputs.append(mixed_out.reshape(NEW, BLOCKS, COLS))
    return jnp.stack(outputs, 0)
```

```python
import functools
import math

import jax
import jax.numpy as jnp
from jax import lax
from jax.experimental import pallas as pl
from jax.experimental.pallas import tpu as pltpu
from jax.sharding import PartitionSpec as P

HD = 128


masked_score = -1e30


def softmax_terms(scores, visible, value_rows):
    scores = jnp.where(visible, scores, masked_score)
    top_score = jnp.max(scores, axis=-1)
    weights = jnp.where(visible, jnp.exp(scores - top_score[..., None]), 0.0)
    weight_sum = jnp.sum(weights, axis=-1)
    summed = jnp.dot(weights.astype(jnp.bfloat16), value_rows, preferred_element_type=jnp.float32)
    return (top_score, weight_sum, summed)


def masked_terms(query_rows, row_doc, key_rows, value_rows, doc_rows, length, score_scale):
    scores = jnp.dot(query_rows, key_rows.T, preferred_element_type=jnp.float32) * score_scale
    positions = jnp.arange(key_rows.shape[0], dtype=jnp.int32)
    visible = (positions[None, :] < length) & (doc_rows[None, :] == row_doc[:, None])
    return softmax_terms(scores, visible, value_rows)


def join_terms(earlier, later):
    top_score = jnp.maximum(earlier[0], later[0])
    early_factor = jnp.exp(earlier[0] - top_score)
    late_factor = jnp.exp(later[0] - top_score)
    weight_sum = earlier[1] * early_factor + later[1] * late_factor
    summed = earlier[2] * early_factor[..., None] + later[2] * late_factor[..., None]
    return (top_score, weight_sum, summed)


def local(
    queries,
    new_keys,
    new_values,
    cache_keys,
    cache_values,
    keep_lengths,
    cache_doc,
    new_doc,
    out_weight,
):
    score_scale = HD ** (-0.5)
    tok_rows = queries.shape[1]
    local_heads = queries.shape[2] // HD
    local_kv = cache_keys.shape[2] // HD
    head_group = local_heads // local_kv
    cache_rows = cache_keys.shape[1]
    all_queries, all_keys, all_values, all_doc = (
        lax.all_gather(queries, "seq", axis=1, tiled=True),
        lax.all_gather(new_keys, "seq", axis=1, tiled=True),
        lax.all_gather(new_values, "seq", axis=1, tiled=True),
        lax.all_gather(new_doc, "seq", axis=1, tiled=True),
    )
    pack_len = all_queries.shape[1]
    query_rows = all_queries[0].reshape(pack_len, local_kv, head_group, HD).transpose(1, 0, 2, 3)
    row_doc = jnp.repeat(all_doc[0], head_group)
    block_size = math.gcd(pack_len * head_group, 1024)
    block_count = pack_len * head_group // block_size
    query_blocks = query_rows.reshape(local_kv * block_count, block_size, HD)
    doc_blocks = jnp.tile(row_doc.reshape(block_count, block_size), (local_kv, 1))
    head_ids = jnp.repeat(jnp.arange(local_kv, dtype=jnp.int32), block_count)
    key_heads = cache_keys[0].reshape(cache_rows, local_kv, HD).transpose(1, 0, 2)
    value_heads = cache_values[0].reshape(cache_rows, local_kv, HD).transpose(1, 0, 2)
    doc_rows = cache_doc[0]
    length = keep_lengths[0, 0]

    def block_terms(inputs):
        query_block, block_doc, head_index = inputs
        key_rows = lax.dynamic_index_in_dim(key_heads, head_index, 0, keepdims=False)
        value_rows = lax.dynamic_index_in_dim(value_heads, head_index, 0, keepdims=False)
        return masked_terms(
            query_block, block_doc, key_rows, value_rows, doc_rows, length, score_scale
        )

    block_tops, block_sums, block_partial = lax.map(
        block_terms, (query_blocks, doc_blocks, head_ids)
    )
    cache_top = block_tops.reshape(local_kv, pack_len, head_group)
    cache_sum = block_sums.reshape(local_kv, pack_len, head_group)
    cache_partial = block_partial.reshape(local_kv, pack_len, head_group, HD)
    my_start = lax.axis_index("seq") * tok_rows
    shares = (
        lax.all_to_all(cache_top[None], "seq", split_axis=2, concat_axis=0, tiled=True),
        lax.all_to_all(cache_sum[None], "seq", split_axis=2, concat_axis=0, tiled=True),
        lax.all_to_all(cache_partial[None], "seq", split_axis=2, concat_axis=0, tiled=True),
    )
    overall_top = jnp.max(shares[0], axis=0)
    factors = jnp.exp(shares[0] - overall_top[None])
    merged = (
        overall_top,
        jnp.sum(shares[1] * factors, 0),
        jnp.sum(shares[2] * factors[..., None], 0),
    )
    own_queries = (
        queries[0]
        .reshape(tok_rows, local_kv, head_group, HD)
        .transpose(1, 0, 2, 3)
        .reshape(local_kv, tok_rows * head_group, HD)
    )
    fresh_keys = all_keys[0].reshape(pack_len, local_kv, HD).transpose(1, 0, 2)
    fresh_values = all_values[0].reshape(pack_len, local_kv, HD).transpose(1, 0, 2)
    scores = (
        jnp.einsum("gqd,gkd->gqk", own_queries, fresh_keys, preferred_element_type=jnp.float32)
        * score_scale
    )
    row_token = my_start + jnp.arange(tok_rows * head_group, dtype=jnp.int32) // head_group
    own_doc = jnp.repeat(new_doc[0], head_group)
    key_index = jnp.arange(pack_len, dtype=jnp.int32)
    visible = (
        (key_index[None, :] <= row_token[:, None]) & (all_doc[0][None, :] == own_doc[:, None])
    )[None]
    scores = jnp.where(visible, scores, masked_score)
    fresh_top = jnp.max(scores, axis=-1)
    weights = jnp.where(visible, jnp.exp(scores - fresh_top[..., None]), 0.0)
    fresh_sum = jnp.sum(weights, axis=-1)
    fresh_partial = jnp.einsum(
        "gqk,gkd->gqd",
        weights.astype(jnp.bfloat16),
        fresh_values,
        preferred_element_type=jnp.float32,
    )
    fresh = (
        fresh_top.reshape(local_kv, tok_rows, head_group),
        fresh_sum.reshape(local_kv, tok_rows, head_group),
        fresh_partial.reshape(local_kv, tok_rows, head_group, HD),
    )
    final = join_terms(merged, fresh)
    attended = (
        (final[2] / final[1][..., None])
        .transpose(1, 0, 2, 3)
        .reshape(1, tok_rows, local_heads * HD)
        .astype(jnp.bfloat16)
    )
    partial_cols = jnp.einsum(
        "ptf,fc->ptc",
        lax.all_gather(attended, "dp", axis=0, tiled=True),
        out_weight,
        preferred_element_type=jnp.float32,
    )
    summed_cols = lax.psum_scatter(partial_cols, "tensor", scatter_dimension=2, tiled=True).astype(
        jnp.bfloat16
    )
    return lax.all_to_all(summed_cols[:, :, None, :], "dp", split_axis=0, concat_axis=2, tiled=True)


MESH = pl.DeviceIdType.MESH
LANES = 128


def fused_kernel(
    n_seq,
    n_dp,
    group,
    q_ref,
    nk_ref,
    nv_ref,
    ck_ref,
    cv_ref,
    meta_ref,
    w_ref,
    out_ref,
    qb,
    kb,
    vb,
    mb,
    att,
    rows,
    wv,
    acc,
    half_out,
    half_in,
    fin,
    z_send,
    z_recv,
    att_send,
    att_recv,
    dp_send,
    dp_recv,
    t_send,
    t_recv,
    o_send,
    o_recv,
    w_sem,
):
    s = lax.axis_index("seq")
    p = lax.axis_index("dp")
    t = lax.axis_index("tensor")
    toks = qb.shape[1]
    width = group * HD
    slots = ck_ref.shape[1]
    keys = kb.shape[1]
    cols = w_ref.shape[1]
    half = cols // 2
    scale2 = HD ** (-0.5) * math.log2(math.e)

    def z_parts(d, k):
        own = pl.ds(pl.multiple_of(d * HD, HD), HD)
        wide = pl.ds(pl.multiple_of(d * width, width), width)
        return (
            (meta_ref, mb.at[k]),
            (ck_ref.at[0, :, own], kb.at[k, pl.ds(0, slots), :]),
            (cv_ref.at[0, :, own], vb.at[k, pl.ds(0, slots), :]),
            (nk_ref.at[0, :, own], kb.at[k, pl.ds(slots, toks), :]),
            (nv_ref.at[0, :, own], vb.at[k, pl.ds(slots, toks), :]),
            (q_ref.at[0, :, wide], qb.at[k]),
        )

    def z_copy(kind, k):
        d = lax.rem(s + k, n_seq)
        src, dst = z_parts(d, k)[kind]
        return pltpu.make_async_remote_copy(
            src_ref=src,
            dst_ref=dst,
            send_sem=z_send.at[kind, k],
            recv_sem=z_recv.at[kind, k],
            device_id={"seq": d},
            device_id_type=MESH,
        )

    def own_copy(kind):
        src, dst = z_parts(s, 0)[kind]
        return pltpu.make_async_copy(src, dst, z_recv.at[kind, 0])

    def att_copy(k):
        return pltpu.make_async_remote_copy(
            src_ref=att.at[k],
            dst_ref=rows.at[k, 0],
            send_sem=att_send.at[k],
            recv_sem=att_recv.at[k],
            device_id={"seq": lax.rem(s + n_seq - k, n_seq)},
            device_id_type=MESH,
        )

    def dp_copy(k, j):
        return pltpu.make_async_remote_copy(
            src_ref=rows.at[k, 0],
            dst_ref=rows.at[k, j],
            send_sem=dp_send.at[k, j],
            recv_sem=dp_recv.at[k, j],
            device_id={"dp": lax.rem(p + j, n_dp)},
            device_id_type=MESH,
        )

    def out_copy(j):
        return pltpu.make_async_remote_copy(
            src_ref=fin.at[j],
            dst_ref=out_ref.at[p],
            send_sem=o_send.at[j],
            recv_sem=o_recv.at[j],
            device_id={"dp": lax.rem(p + n_dp - j, n_dp)},
            device_id_type=MESH,
        )

    def w_copy(k):
        part = pl.ds(pl.multiple_of(lax.rem(s + k, n_seq) * width, width), width)
        return pltpu.make_async_copy(w_ref.at[part, :], wv.at[k], w_sem.at[k])

    barrier = pltpu.get_barrier_semaphore()
    for k in range(1, n_seq):
        pl.semaphore_signal(
            barrier, inc=1, device_id={"seq": lax.rem(s + k, n_seq)}, device_id_type=MESH
        )
    for j in range(1, n_dp):
        pl.semaphore_signal(
            barrier, inc=1, device_id={"dp": lax.rem(p + j, n_dp)}, device_id_type=MESH
        )
    pl.semaphore_signal(barrier, inc=1, device_id={"tensor": 1 - t}, device_id_type=MESH)
    for kind in range(6):
        own_copy(kind).start()
    for k in range(n_seq):
        kb[k, slots + toks :, :] = jnp.zeros((keys - slots - toks, HD), kb.dtype)
        vb[k, slots + toks :, :] = jnp.zeros((keys - slots - toks, HD), vb.dtype)
    pl.semaphore_wait(barrier, n_seq + n_dp - 1)

    for kinds in ((0, 1, 2, 3, 4), (5,)):
        for k in range(1, n_seq):
            for kind in kinds:
                z_copy(kind, k).start()
    for k in range(n_seq):
        w_copy(k).start()
    for kind in range(5):
        own_copy(kind).wait()
    for k in range(1, n_seq):
        for kind in range(5):
            z_copy(kind, k).wait_recv()

    lane = lax.broadcasted_iota(jnp.int32, (toks, keys), 1)
    token = lax.broadcasted_iota(jnp.int32, (toks, keys), 0)
    step_heads = max(1, group // 2)

    def attend(k):
        first = lax.rem(s + n_seq - k, n_seq) * toks
        doc_row = mb[k, 0:1, slots : slots + LANES]
        doc_col = jnp.transpose(jnp.broadcast_to(doc_row, (LANES, LANES)))[:toks, 0:1]

        @pl.loop(0, group // step_heads)
        def _(part):
            base = pl.multiple_of(part * (step_heads * HD), step_heads * HD)
            queries = jnp.concatenate(
                [
                    qb[k, :, pl.ds(pl.multiple_of(base + i * HD, HD), HD)]
                    for i in range(step_heads)
                ],
                axis=0,
            )
            top = weight_sum = summed = None
            for j in range(n_seq):
                scores = lax.dot_general(
                    queries,
                    kb[j],
                    (((1,), (1,)), ((), ())),
                    preferred_element_type=jnp.float32,
                )
                fresh_at = lax.rem(s + n_seq - j, n_seq) * toks - slots
                seen = (mb[j, 0:1, :] == doc_col) & (
                    (lane < slots) | (lane + fresh_at <= token + first)
                )
                bias = jnp.where(seen, 0.0, masked_score)
                scores = scores + jnp.concatenate([bias] * step_heads, axis=0)
                group_top = jnp.max(scores, axis=-1, keepdims=True)
                new_top = group_top if top is None else jnp.maximum(top, group_top)
                weights = jnp.exp2((scores - new_top) * scale2)
                part_sum = jnp.sum(weights, axis=-1, keepdims=True)
                part_out = jnp.dot(
                    weights.astype(jnp.bfloat16), vb[j], preferred_element_type=jnp.float32
                )
                if top is None:
                    weight_sum, summed = part_sum, part_out
                else:
                    factor = jnp.exp2((top - new_top) * scale2)
                    weight_sum = weight_sum * factor + part_sum
                    summed = summed * factor + part_out
                top = new_top
            result = (summed / weight_sum).astype(jnp.bfloat16)
            for i in range(step_heads):
                att[k, :, pl.ds(pl.multiple_of(base + i * HD, HD), HD)] = result[
                    i * toks : (i + 1) * toks
                ]

    @pl.loop(0, n_seq)
    def _(k):
        @pl.when(k == 0)
        def _():
            own_copy(5).wait()

        for other in range(1, n_seq):

            @pl.when(k == other)
            def _():
                z_copy(5, other).wait_recv()

        attend(k)

        @pl.when(k == 0)
        def _():
            rows[0, 0] = att[0]
            for j in range(1, n_dp):
                dp_copy(0, j).start()

        for other in range(1, n_seq):

            @pl.when(k == other)
            def _():
                att_copy(other).start()

    tile = math.gcd(half, 512)

    def project(k, n):
        lhs = rows[k].reshape(n_dp * toks, width)
        at = pl.ds(pl.multiple_of(n, tile), tile)
        product = jnp.dot(lhs, wv[k, :, at], preferred_element_type=jnp.float32)
        if k > 0:
            product = product + acc[:, at]
        return product, at

    def project_all(k):
        w_copy(k).wait()
        for j in range(1, n_dp):
            dp_copy(k, j).wait_recv()

        @pl.loop(0, cols // tile)
        def _(n):
            product, at = project(k, n * tile)
            acc[:, at] = product

    def forward(k):
        att_copy(k).wait_recv()
        for j in range(1, n_dp):
            dp_copy(k, j).start()

    project_all(0)
    for k in range(1, n_seq):
        forward(k)
    for k in range(1, n_seq - 1):
        project_all(k)
    last = n_seq - 1
    w_copy(last).wait()
    for j in range(1, n_dp):
        dp_copy(last, j).wait_recv()
    theirs, mine = (1 - t) * half, t * half

    @pl.loop(0, half // tile)
    def _(n):
        product, _ = project(last, theirs + n * tile)
        half_out[:, pl.ds(pl.multiple_of(n * tile, tile), tile)] = product.astype(jnp.bfloat16)

    across = pltpu.make_async_remote_copy(
        src_ref=half_out,
        dst_ref=half_in,
        send_sem=t_send,
        recv_sem=t_recv,
        device_id={"tensor": 1 - t},
        device_id_type=MESH,
    )
    across.start()

    @pl.loop(0, half // tile)
    def _(n):
        product, at = project(last, mine + n * tile)
        acc[:, at] = product

    across.wait_recv()
    own_half = pl.ds(pl.multiple_of(mine, half), half)
    for j in (*range(1, n_dp), 0):
        band = pl.ds(j * toks, toks)
        total = acc[band, own_half] + half_in[band, :].astype(jnp.float32)
        fin[j] = total.astype(jnp.bfloat16)
        if j:
            out_copy(j).start()
    keep = pltpu.make_async_copy(fin.at[0], out_ref.at[p], o_send.at[0])
    keep.start()

    for k in range(1, n_seq):
        for kind in range(6):
            z_copy(kind, k).wait_send()
        att_copy(k).wait_send()
    for k in range(n_seq):
        for j in range(1, n_dp):
            dp_copy(k, j).wait_send()
    across.wait_send()
    keep.wait()
    for j in range(1, n_dp):
        out_copy(j).wait()


def fused(
    n_seq,
    n_dp,
    queries,
    new_keys,
    new_values,
    cache_keys,
    cache_values,
    keep_lengths,
    cache_doc,
    new_doc,
    out_weight,
):
    toks = queries.shape[1]
    slots = cache_keys.shape[1]
    cols = out_weight.shape[1]
    group = queries.shape[2] // cache_keys.shape[2]
    width = group * HD
    keys = slots + pl.cdiv(toks, LANES) * LANES
    position = jnp.arange(slots, dtype=jnp.int32)
    kept_doc = jnp.where(position < keep_lengths[0, 0], cache_doc[0], -1)
    pad = jnp.full((keys - slots - toks,), -2, jnp.int32)
    meta = jnp.concatenate([kept_doc, new_doc[0], pad]).astype(jnp.float32)
    meta = jnp.broadcast_to(meta[None], (8, keys))
    dma = pltpu.SemaphoreType.DMA
    bf16 = jnp.bfloat16
    blocks = pl.pallas_call(
        functools.partial(fused_kernel, n_seq, n_dp, group),
        out_shape=jax.ShapeDtypeStruct((n_dp, toks, cols // 2), bf16),
        in_specs=[pl.BlockSpec(memory_space=pl.ANY)] * 7,
        out_specs=pl.BlockSpec(memory_space=pl.ANY),
        scratch_shapes=[
            pltpu.VMEM((n_seq, toks, width), bf16),
            pltpu.VMEM((n_seq, keys, HD), bf16),
            pltpu.VMEM((n_seq, keys, HD), bf16),
            pltpu.VMEM((n_seq, 8, keys), jnp.float32),
            pltpu.VMEM((n_seq, toks, width), bf16),
            pltpu.VMEM((n_seq, n_dp, toks, width), bf16),
            pltpu.VMEM((n_seq, width, cols), bf16),
            pltpu.VMEM((n_dp * toks, cols), jnp.float32),
            pltpu.VMEM((n_dp * toks, cols // 2), bf16),
            pltpu.VMEM((n_dp * toks, cols // 2), bf16),
            pltpu.VMEM((n_dp, toks, cols // 2), bf16),
            dma((6, n_seq)),
            dma((6, n_seq)),
            dma((n_seq,)),
            dma((n_seq,)),
            dma((n_seq, n_dp)),
            dma((n_seq, n_dp)),
            dma,
            dma,
            dma((n_dp,)),
            dma((n_dp,)),
            dma((n_seq,)),
        ],
        compiler_params=pltpu.CompilerParams(
            collective_id=0, has_side_effects=True, vmem_limit_bytes=56 << 20
        ),
    )(queries, new_keys, new_values, cache_keys, cache_values, meta, out_weight)
    return blocks.transpose(1, 0, 2)[None]


def placed_local(mesh, *args):
    n_seq, n_dp, n_tensor = (mesh.shape[axis] for axis in ("seq", "dp", "tensor"))
    queries, cache_keys = args[0], args[3]
    local_kv = cache_keys.shape[2] // HD
    if local_kv == n_seq and n_tensor == 2 and queries.shape[1] <= LANES:
        return fused(n_seq, n_dp, *args)
    return local(*args)


def solution(mesh):
    placed = (
        P("dp", "seq", "tensor"),
        P("dp", "seq", "tensor"),
        P("dp", "seq", "tensor"),
        P("dp", "seq", "tensor"),
        P("dp", "seq", "tensor"),
        P("dp", "seq"),
        P("dp", "seq"),
        P("dp", "seq"),
        P("tensor", "dp"),
    )
    return jax.shard_map(
        functools.partial(placed_local, mesh),
        mesh=mesh,
        in_specs=placed,
        out_specs=P("dp", "seq", None, "tensor"),
        check_vma=False,
    )
```

```python
import functools
import math

import jax
import jax.numpy as jnp
from jax import lax
from jax.experimental import pallas as pl
from jax.experimental.pallas import tpu as pltpu
from jax.sharding import PartitionSpec as P

HD = 128


masked_score = -1e30


def softmax_terms(scores, visible, value_rows):
    scores = jnp.where(visible, scores, masked_score)
    top_score = jnp.max(scores, axis=-1)
    weights = jnp.where(visible, jnp.exp(scores - top_score[..., None]), 0.0)
    weight_sum = jnp.sum(weights, axis=-1)
    summed = jnp.dot(weights.astype(jnp.bfloat16), value_rows, preferred_element_type=jnp.float32)
    return (top_score, weight_sum, summed)


def masked_terms(query_rows, row_doc, key_rows, value_rows, doc_rows, length, score_scale):
    scores = jnp.dot(query_rows, key_rows.T, preferred_element_type=jnp.float32) * score_scale
    positions = jnp.arange(key_rows.shape[0], dtype=jnp.int32)
    visible = (positions[None, :] < length) & (doc_rows[None, :] == row_doc[:, None])
    return softmax_terms(scores, visible, value_rows)


def join_terms(earlier, later):
    top_score = jnp.maximum(earlier[0], later[0])
    early_factor = jnp.exp(earlier[0] - top_score)
    late_factor = jnp.exp(later[0] - top_score)
    weight_sum = earlier[1] * early_factor + later[1] * late_factor
    summed = earlier[2] * early_factor[..., None] + later[2] * late_factor[..., None]
    return (top_score, weight_sum, summed)


def local(
    queries,
    new_keys,
    new_values,
    cache_keys,
    cache_values,
    keep_lengths,
    cache_doc,
    new_doc,
    out_weight,
):
    score_scale = HD ** (-0.5)
    tok_rows = queries.shape[1]
    local_heads = queries.shape[2] // HD
    local_kv = cache_keys.shape[2] // HD
    head_group = local_heads // local_kv
    cache_rows = cache_keys.shape[1]
    all_queries, all_keys, all_values, all_doc = (
        lax.all_gather(queries, "seq", axis=1, tiled=True),
        lax.all_gather(new_keys, "seq", axis=1, tiled=True),
        lax.all_gather(new_values, "seq", axis=1, tiled=True),
        lax.all_gather(new_doc, "seq", axis=1, tiled=True),
    )
    pack_len = all_queries.shape[1]
    query_rows = all_queries[0].reshape(pack_len, local_kv, head_group, HD).transpose(1, 0, 2, 3)
    row_doc = jnp.repeat(all_doc[0], head_group)
    block_size = math.gcd(pack_len * head_group, 1024)
    block_count = pack_len * head_group // block_size
    query_blocks = query_rows.reshape(local_kv * block_count, block_size, HD)
    doc_blocks = jnp.tile(row_doc.reshape(block_count, block_size), (local_kv, 1))
    head_ids = jnp.repeat(jnp.arange(local_kv, dtype=jnp.int32), block_count)
    key_heads = cache_keys[0].reshape(cache_rows, local_kv, HD).transpose(1, 0, 2)
    value_heads = cache_values[0].reshape(cache_rows, local_kv, HD).transpose(1, 0, 2)
    doc_rows = cache_doc[0]
    length = keep_lengths[0, 0]

    def block_terms(inputs):
        query_block, block_doc, head_index = inputs
        key_rows = lax.dynamic_index_in_dim(key_heads, head_index, 0, keepdims=False)
        value_rows = lax.dynamic_index_in_dim(value_heads, head_index, 0, keepdims=False)
        return masked_terms(
            query_block, block_doc, key_rows, value_rows, doc_rows, length, score_scale
        )

    block_tops, block_sums, block_partial = lax.map(
        block_terms, (query_blocks, doc_blocks, head_ids)
    )
    cache_top = block_tops.reshape(local_kv, pack_len, head_group)
    cache_sum = block_sums.reshape(local_kv, pack_len, head_group)
    cache_partial = block_partial.reshape(local_kv, pack_len, head_group, HD)
    my_start = lax.axis_index("seq") * tok_rows
    shares = (
        lax.all_to_all(cache_top[None], "seq", split_axis=2, concat_axis=0, tiled=True),
        lax.all_to_all(cache_sum[None], "seq", split_axis=2, concat_axis=0, tiled=True),
        lax.all_to_all(cache_partial[None], "seq", split_axis=2, concat_axis=0, tiled=True),
    )
    overall_top = jnp.max(shares[0], axis=0)
    factors = jnp.exp(shares[0] - overall_top[None])
    merged = (
        overall_top,
        jnp.sum(shares[1] * factors, 0),
        jnp.sum(shares[2] * factors[..., None], 0),
    )
    own_queries = (
        queries[0]
        .reshape(tok_rows, local_kv, head_group, HD)
        .transpose(1, 0, 2, 3)
        .reshape(local_kv, tok_rows * head_group, HD)
    )
    fresh_keys = all_keys[0].reshape(pack_len, local_kv, HD).transpose(1, 0, 2)
    fresh_values = all_values[0].reshape(pack_len, local_kv, HD).transpose(1, 0, 2)
    scores = (
        jnp.einsum("gqd,gkd->gqk", own_queries, fresh_keys, preferred_element_type=jnp.float32)
        * score_scale
    )
    row_token = my_start + jnp.arange(tok_rows * head_group, dtype=jnp.int32) // head_group
    own_doc = jnp.repeat(new_doc[0], head_group)
    key_index = jnp.arange(pack_len, dtype=jnp.int32)
    visible = (
        (key_index[None, :] <= row_token[:, None]) & (all_doc[0][None, :] == own_doc[:, None])
    )[None]
    scores = jnp.where(visible, scores, masked_score)
    fresh_top = jnp.max(scores, axis=-1)
    weights = jnp.where(visible, jnp.exp(scores - fresh_top[..., None]), 0.0)
    fresh_sum = jnp.sum(weights, axis=-1)
    fresh_partial = jnp.einsum(
        "gqk,gkd->gqd",
        weights.astype(jnp.bfloat16),
        fresh_values,
        preferred_element_type=jnp.float32,
    )
    fresh = (
        fresh_top.reshape(local_kv, tok_rows, head_group),
        fresh_sum.reshape(local_kv, tok_rows, head_group),
        fresh_partial.reshape(local_kv, tok_rows, head_group, HD),
    )
    final = join_terms(merged, fresh)
    attended = (
        (final[2] / final[1][..., None])
        .transpose(1, 0, 2, 3)
        .reshape(1, tok_rows, local_heads * HD)
        .astype(jnp.bfloat16)
    )
    partial_cols = jnp.einsum(
        "ptf,fc->ptc",
        lax.all_gather(attended, "dp", axis=0, tiled=True),
        out_weight,
        preferred_element_type=jnp.float32,
    )
    summed_cols = lax.psum_scatter(partial_cols, "tensor", scatter_dimension=2, tiled=True).astype(
        jnp.bfloat16
    )
    return lax.all_to_all(summed_cols[:, :, None, :], "dp", split_axis=0, concat_axis=2, tiled=True)


MESH = pl.DeviceIdType.MESH
LANES = 128
PARTS = 2


def fused_kernel(
    n_seq,
    n_dp,
    group,
    q_ref,
    nk_ref,
    nv_ref,
    ck_ref,
    cv_ref,
    keep_ref,
    cache_doc_ref,
    new_doc_ref,
    w_ref,
    out_ref,
    qb,
    kb,
    vb,
    mb,
    att,
    rows,
    wv,
    acc,
    half_out,
    half_in,
    fin,
    z_send,
    z_recv,
    att_send,
    att_recv,
    dp_send,
    dp_recv,
    t_send,
    t_recv,
    o_send,
    o_recv,
    w_sem,
):
    s = lax.axis_index("seq")
    p = lax.axis_index("dp")
    t = lax.axis_index("tensor")
    toks = qb.shape[1]
    width = group * HD
    slots = ck_ref.shape[1]
    keys = kb.shape[1]
    cols = w_ref.shape[1]
    half = cols // 2
    tile = half // fin.shape[0]
    depth = width // PARTS
    scale2 = HD ** (-0.5) * math.log2(math.e)

    def z_parts(d, k):
        own = pl.ds(pl.multiple_of(d * HD, HD), HD)
        wide = pl.ds(pl.multiple_of(d * width, width), width)
        return (
            (mb.at[0], mb.at[k]),
            (ck_ref.at[0, :, own], kb.at[k, pl.ds(0, slots), :]),
            (cv_ref.at[0, :, own], vb.at[k, pl.ds(0, slots), :]),
            (nk_ref.at[0, :, own], kb.at[k, pl.ds(slots, toks), :]),
            (nv_ref.at[0, :, own], vb.at[k, pl.ds(slots, toks), :]),
            (q_ref.at[0, :, wide], qb.at[k]),
        )

    def z_copy(kind, k):
        d = lax.rem(s + k, n_seq)
        src, dst = z_parts(d, k)[kind]
        return pltpu.make_async_remote_copy(
            src_ref=src,
            dst_ref=dst,
            send_sem=z_send.at[kind, k],
            recv_sem=z_recv.at[kind, k],
            device_id={"seq": d},
            device_id_type=MESH,
        )

    def own_copy(kind):
        src, dst = z_parts(s, 0)[kind]
        return pltpu.make_async_copy(src, dst, z_recv.at[kind, 0])

    def att_copy(k, part):
        return pltpu.make_async_remote_copy(
            src_ref=att.at[k, part],
            dst_ref=rows.at[k, part, 0],
            send_sem=att_send.at[k, part],
            recv_sem=att_recv.at[k, part],
            device_id={"seq": lax.rem(s + n_seq - k, n_seq)},
            device_id_type=MESH,
        )

    def dp_copy(k, part, j):
        return pltpu.make_async_remote_copy(
            src_ref=rows.at[k, part, 0],
            dst_ref=rows.at[k, part, j],
            send_sem=dp_send.at[k, part, j],
            recv_sem=dp_recv.at[k, part, j],
            device_id={"dp": lax.rem(p + j, n_dp)},
            device_id_type=MESH,
        )

    def out_copy(n, j):
        return pltpu.make_async_remote_copy(
            src_ref=fin.at[n, j],
            dst_ref=out_ref.at[p, :, pl.ds(n * tile, tile)],
            send_sem=o_send.at[n, j],
            recv_sem=o_recv.at[n, j],
            device_id={"dp": lax.rem(p + n_dp - j, n_dp)},
            device_id_type=MESH,
        )

    def w_copy(k):
        part = pl.ds(pl.multiple_of(lax.rem(s + k, n_seq) * width, width), width)
        return pltpu.make_async_copy(w_ref.at[part, :], wv.at[k], w_sem.at[k])

    barrier = pltpu.get_barrier_semaphore()
    for k in range(1, n_seq):
        pl.semaphore_signal(
            barrier, inc=1, device_id={"seq": lax.rem(s + k, n_seq)}, device_id_type=MESH
        )
    for j in range(1, n_dp):
        pl.semaphore_signal(
            barrier, inc=1, device_id={"dp": lax.rem(p + j, n_dp)}, device_id_type=MESH
        )
    pl.semaphore_signal(barrier, inc=1, device_id={"tensor": 1 - t}, device_id_type=MESH)
    for kind in range(1, 6):
        own_copy(kind).start()
    place = lax.broadcasted_iota(jnp.int32, (1, slots), 1)
    kept_doc = jnp.where(place < keep_ref[0, 0], cache_doc_ref[...], -1)
    mb[0, :, :slots] = kept_doc.astype(jnp.float32)
    mb[0, :, slots:] = jnp.full((1, keys - slots), -2.0, jnp.float32)
    mb[0, :, slots : slots + toks] = new_doc_ref[...].astype(jnp.float32)
    for k in range(n_seq):
        kb[k, slots + toks :, :] = jnp.zeros((keys - slots - toks, HD), kb.dtype)
        vb[k, slots + toks :, :] = jnp.zeros((keys - slots - toks, HD), vb.dtype)
    pl.semaphore_wait(barrier, n_seq + n_dp - 1)

    for kinds in ((1, 2, 3, 4, 0), (5,)):
        for k in range(1, n_seq):
            for kind in kinds:
                z_copy(kind, k).start()
    for k in range(n_seq):
        w_copy(k).start()

    lane = lax.broadcasted_iota(jnp.int32, (toks, keys), 1)
    token = lax.broadcasted_iota(jnp.int32, (toks, keys), 0)
    step_heads = group // PARTS

    def attend(k, part, wait_shards):
        first = lax.rem(s + n_seq - k, n_seq) * toks
        base = part * depth
        queries = jnp.concatenate(
            [qb[k, :, pl.ds(pl.multiple_of(base + i * HD, HD), HD)] for i in range(step_heads)],
            axis=0,
        )
        doc_row = mb[k, :, slots : slots + LANES]
        doc_col = jnp.transpose(jnp.broadcast_to(doc_row, (LANES, LANES)))[:toks, 0:1]
        top = weight_sum = summed = None
        for j in range(n_seq):
            if wait_shards:
                for kind in range(5):
                    if j:
                        z_copy(kind, j).wait_recv()
                    elif kind:
                        own_copy(kind).wait()
            scores = lax.dot_general(
                queries,
                kb[j],
                (((1,), (1,)), ((), ())),
                preferred_element_type=jnp.float32,
            )
            fresh_at = lax.rem(s + n_seq - j, n_seq) * toks - slots
            seen = (mb[j] == doc_col) & ((lane < slots) | (lane + fresh_at <= token + first))
            bias = jnp.where(seen, 0.0, masked_score)
            scores = scores + jnp.concatenate([bias] * step_heads, axis=0)
            group_top = jnp.max(scores, axis=-1, keepdims=True)
            new_top = group_top if top is None else jnp.maximum(top, group_top)
            weights = jnp.exp2((scores - new_top) * scale2)
            part_sum = jnp.sum(weights, axis=-1, keepdims=True)
            part_out = jnp.dot(
                weights.astype(jnp.bfloat16), vb[j], preferred_element_type=jnp.float32
            )
            if top is None:
                weight_sum, summed = part_sum, part_out
            else:
                factor = jnp.exp2((top - new_top) * scale2)
                weight_sum = weight_sum * factor + part_sum
                summed = summed * factor + part_out
            top = new_top
        result = (summed / weight_sum).astype(jnp.bfloat16)
        for i in range(step_heads):
            piece = result[i * toks : (i + 1) * toks]
            if wait_shards is None:
                att[k, part, :, i * HD : (i + 1) * HD] = piece
            else:
                rows[0, part, 0, :, i * HD : (i + 1) * HD] = piece

    def forward(k, part):
        if k:
            att_copy(k, part).wait_recv()
        for j in range(1, n_dp):
            dp_copy(k, part, j).start()

    own_copy(5).wait()
    for part in range(PARTS):
        attend(0, part, part == 0)
        forward(0, part)
    for k in range(1, n_seq):
        z_copy(5, k).wait_recv()

        @pl.loop(0, PARTS)
        def _(part):
            attend(k, part, None)
            att_copy(k, part).start()

        if k > 1:
            for part in range(PARTS):
                forward(k - 1, part)

    def project(k, part, n):
        lhs = rows[k, part].reshape(n_dp * toks, depth)
        at = pl.ds(pl.multiple_of(n, tile), tile)
        deep = pl.ds(part * depth, depth)
        product = jnp.dot(lhs, wv[k, deep, at], preferred_element_type=jnp.float32)
        if k or part:
            product = product + acc[:, at]
        return product, at

    def ready(k, part):
        if part == 0:
            w_copy(k).wait()
        for j in range(1, n_dp):
            dp_copy(k, part, j).wait_recv()

    def project_all(k, part):
        ready(k, part)

        @pl.loop(0, cols // tile)
        def _(n):
            product, at = project(k, part, n * tile)
            acc[:, at] = product

    last = (n_seq - 1, PARTS - 1)
    project_all(0, 0)
    forward(last[0], 0)
    project_all(0, 1)
    for part in range(1, PARTS):
        forward(last[0], part)
    for k in range(1, n_seq):
        for part in range(PARTS):
            if (k, part) != last:
                project_all(k, part)
    ready(*last)
    theirs, mine = (1 - t) * half, t * half

    def across(n):
        return pltpu.make_async_remote_copy(
            src_ref=half_out.at[n],
            dst_ref=half_in.at[n],
            send_sem=t_send.at[n],
            recv_sem=t_recv.at[n],
            device_id={"tensor": 1 - t},
            device_id_type=MESH,
        )

    def keep(n):
        there = out_ref.at[p, :, pl.ds(n * tile, tile)]
        return pltpu.make_async_copy(fin.at[n, 0], there, o_send.at[n, 0])

    tiles = half // tile
    for n in range(tiles):
        product, _ = project(*last, theirs + n * tile)
        half_out[n] = product.astype(jnp.bfloat16)
        across(n).start()
    for n in range(tiles):
        product, _ = project(*last, mine + n * tile)
        across(n).wait_recv()
        total = (product + half_in[n].astype(jnp.float32)).astype(jnp.bfloat16)
        for j in (*range(1, n_dp), 0):
            fin[n, j] = total[j * toks : (j + 1) * toks]
            if j:
                out_copy(n, j).start()
        keep(n).start()

    for k in range(1, n_seq):
        for kind in range(6):
            z_copy(kind, k).wait_send()
        for part in range(PARTS):
            att_copy(k, part).wait_send()
    for k in range(n_seq):
        for part in range(PARTS):
            for j in range(1, n_dp):
                dp_copy(k, part, j).wait_send()
    for n in range(tiles):
        across(n).wait_send()
        keep(n).wait()
        for j in range(1, n_dp):
            out_copy(n, j).wait()


def fused(
    n_seq,
    n_dp,
    queries,
    new_keys,
    new_values,
    cache_keys,
    cache_values,
    keep_lengths,
    cache_doc,
    new_doc,
    out_weight,
):
    toks = queries.shape[1]
    slots = cache_keys.shape[1]
    cols = out_weight.shape[1]
    group = queries.shape[2] // cache_keys.shape[2]
    width = group * HD
    keys = slots + pl.cdiv(toks, LANES) * LANES
    tiles = 2
    dma = pltpu.SemaphoreType.DMA
    bf16 = jnp.bfloat16
    blocks = pl.pallas_call(
        functools.partial(fused_kernel, n_seq, n_dp, group),
        out_shape=jax.ShapeDtypeStruct((n_dp, toks, cols // 2), bf16),
        in_specs=[pl.BlockSpec(memory_space=pl.ANY)] * 5
        + [
            pl.BlockSpec(memory_space=pltpu.SMEM),
            pl.BlockSpec(memory_space=pltpu.VMEM),
            pl.BlockSpec(memory_space=pltpu.VMEM),
            pl.BlockSpec(memory_space=pl.ANY),
        ],
        out_specs=pl.BlockSpec(memory_space=pl.ANY),
        scratch_shapes=[
            pltpu.VMEM((n_seq, toks, width), bf16),
            pltpu.VMEM((n_seq, keys, HD), bf16),
            pltpu.VMEM((n_seq, keys, HD), bf16),
            pltpu.VMEM((n_seq, 1, keys), jnp.float32),
            pltpu.VMEM((n_seq, PARTS, toks, width // PARTS), bf16),
            pltpu.VMEM((n_seq, PARTS, n_dp, toks, width // PARTS), bf16),
            pltpu.VMEM((n_seq, width, cols), bf16),
            pltpu.VMEM((n_dp * toks, cols), jnp.float32),
            pltpu.VMEM((tiles, n_dp * toks, cols // 2 // tiles), bf16),
            pltpu.VMEM((tiles, n_dp * toks, cols // 2 // tiles), bf16),
            pltpu.VMEM((tiles, n_dp, toks, cols // 2 // tiles), bf16),
            dma((6, n_seq)),
            dma((6, n_seq)),
            dma((n_seq, PARTS)),
            dma((n_seq, PARTS)),
            dma((n_seq, PARTS, n_dp)),
            dma((n_seq, PARTS, n_dp)),
            dma((tiles,)),
            dma((tiles,)),
            dma((tiles, n_dp)),
            dma((tiles, n_dp)),
            dma((n_seq,)),
        ],
        compiler_params=pltpu.CompilerParams(
            collective_id=0, has_side_effects=True, vmem_limit_bytes=56 << 20
        ),
    )(queries, new_keys, new_values, cache_keys, cache_values, keep_lengths, cache_doc, new_doc, out_weight)
    return blocks.transpose(1, 0, 2)[None]


def placed_local(mesh, *args):
    n_seq, n_dp, n_tensor = (mesh.shape[axis] for axis in ("seq", "dp", "tensor"))
    queries, cache_keys = args[0], args[3]
    local_kv = cache_keys.shape[2] // HD
    if local_kv == n_seq and n_tensor == 2 and queries.shape[1] <= LANES:
        return fused(n_seq, n_dp, *args)
    return local(*args)


def solution(mesh):
    placed = (
        P("dp", "seq", "tensor"),
        P("dp", "seq", "tensor"),
        P("dp", "seq", "tensor"),
        P("dp", "seq", "tensor"),
        P("dp", "seq", "tensor"),
        P("dp", "seq"),
        P("dp", "seq"),
        P("dp", "seq"),
        P("tensor", "dp"),
    )
    return jax.shard_map(
        functools.partial(placed_local, mesh),
        mesh=mesh,
        in_specs=placed,
        out_specs=P("dp", "seq", None, "tensor"),
        check_vma=False,
    )
```

```python
import functools
import math

import jax
import jax.numpy as jnp
from jax import lax
from jax.experimental import pallas as pl
from jax.experimental.pallas import tpu as pltpu
from jax.sharding import PartitionSpec as P

HD = 128


masked_score = -1e30


def softmax_terms(scores, visible, value_rows):
    scores = jnp.where(visible, scores, masked_score)
    top_score = jnp.max(scores, axis=-1)
    weights = jnp.where(visible, jnp.exp(scores - top_score[..., None]), 0.0)
    weight_sum = jnp.sum(weights, axis=-1)
    summed = jnp.dot(weights.astype(jnp.bfloat16), value_rows, preferred_element_type=jnp.float32)
    return (top_score, weight_sum, summed)


def masked_terms(query_rows, row_doc, key_rows, value_rows, doc_rows, length, score_scale):
    scores = jnp.dot(query_rows, key_rows.T, preferred_element_type=jnp.float32) * score_scale
    positions = jnp.arange(key_rows.shape[0], dtype=jnp.int32)
    visible = (positions[None, :] < length) & (doc_rows[None, :] == row_doc[:, None])
    return softmax_terms(scores, visible, value_rows)


def join_terms(earlier, later):
    top_score = jnp.maximum(earlier[0], later[0])
    early_factor = jnp.exp(earlier[0] - top_score)
    late_factor = jnp.exp(later[0] - top_score)
    weight_sum = earlier[1] * early_factor + later[1] * late_factor
    summed = earlier[2] * early_factor[..., None] + later[2] * late_factor[..., None]
    return (top_score, weight_sum, summed)


def local(
    queries,
    new_keys,
    new_values,
    cache_keys,
    cache_values,
    keep_lengths,
    cache_doc,
    new_doc,
    out_weight,
):
    score_scale = HD ** (-0.5)
    tok_rows = queries.shape[1]
    local_heads = queries.shape[2] // HD
    local_kv = cache_keys.shape[2] // HD
    head_group = local_heads // local_kv
    cache_rows = cache_keys.shape[1]
    all_queries, all_keys, all_values, all_doc = (
        lax.all_gather(queries, "seq", axis=1, tiled=True),
        lax.all_gather(new_keys, "seq", axis=1, tiled=True),
        lax.all_gather(new_values, "seq", axis=1, tiled=True),
        lax.all_gather(new_doc, "seq", axis=1, tiled=True),
    )
    pack_len = all_queries.shape[1]
    query_rows = all_queries[0].reshape(pack_len, local_kv, head_group, HD).transpose(1, 0, 2, 3)
    row_doc = jnp.repeat(all_doc[0], head_group)
    block_size = math.gcd(pack_len * head_group, 1024)
    block_count = pack_len * head_group // block_size
    query_blocks = query_rows.reshape(local_kv * block_count, block_size, HD)
    doc_blocks = jnp.tile(row_doc.reshape(block_count, block_size), (local_kv, 1))
    head_ids = jnp.repeat(jnp.arange(local_kv, dtype=jnp.int32), block_count)
    key_heads = cache_keys[0].reshape(cache_rows, local_kv, HD).transpose(1, 0, 2)
    value_heads = cache_values[0].reshape(cache_rows, local_kv, HD).transpose(1, 0, 2)
    doc_rows = cache_doc[0]
    length = keep_lengths[0, 0]

    def block_terms(inputs):
        query_block, block_doc, head_index = inputs
        key_rows = lax.dynamic_index_in_dim(key_heads, head_index, 0, keepdims=False)
        value_rows = lax.dynamic_index_in_dim(value_heads, head_index, 0, keepdims=False)
        return masked_terms(
            query_block, block_doc, key_rows, value_rows, doc_rows, length, score_scale
        )

    block_tops, block_sums, block_partial = lax.map(
        block_terms, (query_blocks, doc_blocks, head_ids)
    )
    cache_top = block_tops.reshape(local_kv, pack_len, head_group)
    cache_sum = block_sums.reshape(local_kv, pack_len, head_group)
    cache_partial = block_partial.reshape(local_kv, pack_len, head_group, HD)
    my_start = lax.axis_index("seq") * tok_rows
    shares = (
        lax.all_to_all(cache_top[None], "seq", split_axis=2, concat_axis=0, tiled=True),
        lax.all_to_all(cache_sum[None], "seq", split_axis=2, concat_axis=0, tiled=True),
        lax.all_to_all(cache_partial[None], "seq", split_axis=2, concat_axis=0, tiled=True),
    )
    overall_top = jnp.max(shares[0], axis=0)
    factors = jnp.exp(shares[0] - overall_top[None])
    merged = (
        overall_top,
        jnp.sum(shares[1] * factors, 0),
        jnp.sum(shares[2] * factors[..., None], 0),
    )
    own_queries = (
        queries[0]
        .reshape(tok_rows, local_kv, head_group, HD)
        .transpose(1, 0, 2, 3)
        .reshape(local_kv, tok_rows * head_group, HD)
    )
    fresh_keys = all_keys[0].reshape(pack_len, local_kv, HD).transpose(1, 0, 2)
    fresh_values = all_values[0].reshape(pack_len, local_kv, HD).transpose(1, 0, 2)
    scores = (
        jnp.einsum("gqd,gkd->gqk", own_queries, fresh_keys, preferred_element_type=jnp.float32)
        * score_scale
    )
    row_token = my_start + jnp.arange(tok_rows * head_group, dtype=jnp.int32) // head_group
    own_doc = jnp.repeat(new_doc[0], head_group)
    key_index = jnp.arange(pack_len, dtype=jnp.int32)
    visible = (
        (key_index[None, :] <= row_token[:, None]) & (all_doc[0][None, :] == own_doc[:, None])
    )[None]
    scores = jnp.where(visible, scores, masked_score)
    fresh_top = jnp.max(scores, axis=-1)
    weights = jnp.where(visible, jnp.exp(scores - fresh_top[..., None]), 0.0)
    fresh_sum = jnp.sum(weights, axis=-1)
    fresh_partial = jnp.einsum(
        "gqk,gkd->gqd",
        weights.astype(jnp.bfloat16),
        fresh_values,
        preferred_element_type=jnp.float32,
    )
    fresh = (
        fresh_top.reshape(local_kv, tok_rows, head_group),
        fresh_sum.reshape(local_kv, tok_rows, head_group),
        fresh_partial.reshape(local_kv, tok_rows, head_group, HD),
    )
    final = join_terms(merged, fresh)
    attended = (
        (final[2] / final[1][..., None])
        .transpose(1, 0, 2, 3)
        .reshape(1, tok_rows, local_heads * HD)
        .astype(jnp.bfloat16)
    )
    partial_cols = jnp.einsum(
        "ptf,fc->ptc",
        lax.all_gather(attended, "dp", axis=0, tiled=True),
        out_weight,
        preferred_element_type=jnp.float32,
    )
    summed_cols = lax.psum_scatter(partial_cols, "tensor", scatter_dimension=2, tiled=True).astype(
        jnp.bfloat16
    )
    return lax.all_to_all(summed_cols[:, :, None, :], "dp", split_axis=0, concat_axis=2, tiled=True)


MESH = pl.DeviceIdType.MESH
LANES = 128
PARTS = 2


def fused_kernel(
    n_seq,
    n_dp,
    group,
    q_ref,
    nk_ref,
    nv_ref,
    ck_ref,
    cv_ref,
    keep_ref,
    cache_doc_ref,
    new_doc_ref,
    w_ref,
    out_ref,
    qb,
    kb,
    vb,
    mb,
    att,
    rows,
    wv,
    acc,
    half_out,
    half_in,
    fin,
    z_send,
    z_recv,
    att_send,
    att_recv,
    dp_send,
    dp_recv,
    t_send,
    t_recv,
    o_send,
    o_recv,
    w_sem,
):
    s = lax.axis_index("seq")
    p = lax.axis_index("dp")
    t = lax.axis_index("tensor")
    part_toks = qb.shape[2]
    toks = PARTS * part_toks
    width = group * HD
    slots = ck_ref.shape[1]
    keys = kb.shape[1]
    cols = w_ref.shape[1]
    half = cols // 2
    tiles = fin.shape[1]
    tile = half // tiles
    scale2 = HD ** (-0.5) * math.log2(math.e)

    def z_parts(d, k):
        own = pl.ds(pl.multiple_of(d * HD, HD), HD)
        wide = pl.ds(pl.multiple_of(d * width, width), width)
        return (
            (mb.at[0], mb.at[k]),
            (ck_ref.at[0, :, own], kb.at[k, pl.ds(0, slots), :]),
            (cv_ref.at[0, :, own], vb.at[k, pl.ds(0, slots), :]),
            (nk_ref.at[0, :, own], kb.at[k, pl.ds(slots, toks), :]),
            (nv_ref.at[0, :, own], vb.at[k, pl.ds(slots, toks), :]),
            *(
                (q_ref.at[0, pl.ds(part * part_toks, part_toks), wide], qb.at[k, part])
                for part in range(PARTS)
            ),
        )

    def z_copy(kind, k):
        d = lax.rem(s + k, n_seq)
        src, dst = z_parts(d, k)[kind]
        return pltpu.make_async_remote_copy(
            src_ref=src,
            dst_ref=dst,
            send_sem=z_send.at[kind, k],
            recv_sem=z_recv.at[kind, k],
            device_id={"seq": d},
            device_id_type=MESH,
        )

    def own_copy(kind):
        src, dst = z_parts(s, 0)[kind]
        return pltpu.make_async_copy(src, dst, z_recv.at[kind, 0])

    def att_copy(k, part):
        return pltpu.make_async_remote_copy(
            src_ref=att.at[k, part],
            dst_ref=rows.at[k, part, 0],
            send_sem=att_send.at[k, part],
            recv_sem=att_recv.at[k, part],
            device_id={"seq": lax.rem(s + n_seq - k, n_seq)},
            device_id_type=MESH,
        )

    def dp_copy(k, part, j):
        return pltpu.make_async_remote_copy(
            src_ref=rows.at[k, part, 0],
            dst_ref=rows.at[k, part, j],
            send_sem=dp_send.at[k, part, j],
            recv_sem=dp_recv.at[k, part, j],
            device_id={"dp": lax.rem(p + j, n_dp)},
            device_id_type=MESH,
        )

    def out_place(part, n):
        return out_ref.at[p, pl.ds(part * part_toks, part_toks), pl.ds(n * tile, tile)]

    def out_copy(part, n, j):
        return pltpu.make_async_remote_copy(
            src_ref=fin.at[part, n, j],
            dst_ref=out_place(part, n),
            send_sem=o_send.at[part, n, j],
            recv_sem=o_recv.at[part, n, j],
            device_id={"dp": lax.rem(p + n_dp - j, n_dp)},
            device_id_type=MESH,
        )

    def w_copy(k):
        part = pl.ds(pl.multiple_of(lax.rem(s + k, n_seq) * width, width), width)
        return pltpu.make_async_copy(w_ref.at[part, :], wv.at[k], w_sem.at[k])

    barrier = pltpu.get_barrier_semaphore()
    for k in range(1, n_seq):
        pl.semaphore_signal(
            barrier, inc=1, device_id={"seq": lax.rem(s + k, n_seq)}, device_id_type=MESH
        )
    for j in range(1, n_dp):
        pl.semaphore_signal(
            barrier, inc=1, device_id={"dp": lax.rem(p + j, n_dp)}, device_id_type=MESH
        )
    pl.semaphore_signal(barrier, inc=1, device_id={"tensor": 1 - t}, device_id_type=MESH)
    for kind in range(1, 5 + PARTS):
        own_copy(kind).start()
    place = lax.broadcasted_iota(jnp.int32, (1, slots), 1)
    kept_doc = jnp.where(place < keep_ref[0, 0], cache_doc_ref[...], -1)
    mb[0, :, :slots] = kept_doc.astype(jnp.float32)
    mb[0, :, slots:] = jnp.full((1, keys - slots), -2.0, jnp.float32)
    mb[0, :, slots : slots + toks] = new_doc_ref[...].astype(jnp.float32)
    for k in range(n_seq):
        kb[k, slots + toks :, :] = jnp.zeros((keys - slots - toks, HD), kb.dtype)
        vb[k, slots + toks :, :] = jnp.zeros((keys - slots - toks, HD), vb.dtype)
    pl.semaphore_wait(barrier, n_seq + n_dp - 1)

    for kinds in ((1, 2, 3, 4, 0), (5,)):
        for k in range(1, n_seq):
            for kind in kinds:
                z_copy(kind, k).start()
    for part in range(1, PARTS):
        z_copy(5 + part, 1).start()
    for k in range(n_seq):
        w_copy(k).start()

    lane = lax.broadcasted_iota(jnp.int32, (part_toks, keys), 1)
    token = lax.broadcasted_iota(jnp.int32, (part_toks, keys), 0)

    def attend(k, part, into, wait_shards=False):
        first = lax.rem(s + n_seq - k, n_seq) * toks + part * part_toks
        queries = jnp.concatenate(
            [qb[k, part, :, i * HD : (i + 1) * HD] for i in range(group)], axis=0
        )
        doc_row = mb[k, :, slots : slots + LANES]
        doc_col = jnp.transpose(jnp.broadcast_to(doc_row, (LANES, LANES)))
        doc_col = doc_col[part * part_toks : (part + 1) * part_toks, 0:1]
        top = weight_sum = summed = None
        for j in range(n_seq):
            if wait_shards:
                for kind in range(5):
                    if j:
                        z_copy(kind, j).wait_recv()
                    elif kind:
                        own_copy(kind).wait()
            scores = lax.dot_general(
                queries,
                kb[j],
                (((1,), (1,)), ((), ())),
                preferred_element_type=jnp.float32,
            )
            fresh_at = lax.rem(s + n_seq - j, n_seq) * toks - slots
            seen = (mb[j] == doc_col) & ((lane < slots) | (lane + fresh_at <= token + first))
            bias = jnp.where(seen, 0.0, masked_score)
            scores = scores + jnp.concatenate([bias] * group, axis=0)
            group_top = jnp.max(scores, axis=-1, keepdims=True)
            new_top = group_top if top is None else jnp.maximum(top, group_top)
            weights = jnp.exp2((scores - new_top) * scale2)
            part_sum = jnp.sum(weights, axis=-1, keepdims=True)
            part_out = jnp.dot(
                weights.astype(jnp.bfloat16), vb[j], preferred_element_type=jnp.float32
            )
            if top is None:
                weight_sum, summed = part_sum, part_out
            else:
                factor = jnp.exp2((top - new_top) * scale2)
                weight_sum = weight_sum * factor + part_sum
                summed = summed * factor + part_out
            top = new_top
        result = (summed / weight_sum).astype(jnp.bfloat16)
        for i in range(group):
            into[:, i * HD : (i + 1) * HD] = result[i * part_toks : (i + 1) * part_toks]

    def forward(k, part):
        for j in range(1, n_dp):
            dp_copy(k, part, j).start()

    def pass_on(k, part):
        att_copy(k, part).wait_recv()
        forward(k, part)

    last = n_seq - 1
    for part in range(PARTS):
        own_copy(5 + part).wait()
        attend(0, part, rows.at[0, part, 0], wait_shards=part == 0)
        forward(0, part)
    for part in range(PARTS):

        @pl.loop(1, n_seq)
        def _(k):
            z_copy(5 + part, k).wait_recv()
            attend(k, part, att.at[k, part])
            att_copy(k, part).start()
            if part == 0:

                @pl.when(k < last)
                def _():
                    for later in range(1, PARTS):
                        z_copy(5 + later, k + 1).start()

            if part:
                pass_on(k, part - 1)

    def project(k, part, n):
        lhs = rows[k, part].reshape(n_dp * part_toks, width)
        at = pl.ds(pl.multiple_of(n, tile), tile)
        product = jnp.dot(lhs, wv[k, :, at], preferred_element_type=jnp.float32)
        if k:
            product = product + acc[part, :, at]
        return product, at

    def ready(k, part):
        if part == 0:
            w_copy(k).wait()
        for j in range(1, n_dp):
            dp_copy(k, part, j).wait_recv()

    def project_all(k, part):
        ready(k, part)

        @pl.loop(0, cols // tile)
        def _(n):
            product, at = project(k, part, n * tile)
            acc[part, :, at] = product

    theirs, mine = (1 - t) * half, t * half

    def across(part, n):
        return pltpu.make_async_remote_copy(
            src_ref=half_out.at[part, n],
            dst_ref=half_in.at[part, n],
            send_sem=t_send.at[part, n],
            recv_sem=t_recv.at[part, n],
            device_id={"tensor": 1 - t},
            device_id_type=MESH,
        )

    def keep(part, n):
        return pltpu.make_async_copy(
            fin.at[part, n, 0], out_place(part, n), o_send.at[part, n, 0]
        )

    def finish(part):
        ready(last, part)
        for n in range(tiles):
            product, _ = project(last, part, theirs + n * tile)
            half_out[part, n] = product.astype(jnp.bfloat16)
            across(part, n).start()
        for n in range(tiles):
            product, _ = project(last, part, mine + n * tile)
            across(part, n).wait_recv()
            total = (product + half_in[part, n].astype(jnp.float32)).astype(jnp.bfloat16)
            for j in (*range(1, n_dp), 0):
                fin[part, n, j] = total[j * part_toks : (j + 1) * part_toks]
                if j:
                    out_copy(part, n, j).start()
            keep(part, n).start()

    for part in range(PARTS):
        for k in range(last):
            project_all(k, part)
            if part == 0:
                pass_on(k + 1, PARTS - 1)
        finish(part)

    for k in range(1, n_seq):
        for kind in range(5 + PARTS):
            z_copy(kind, k).wait_send()
        for part in range(PARTS):
            att_copy(k, part).wait_send()
    for k in range(n_seq):
        for part in range(PARTS):
            for j in range(1, n_dp):
                dp_copy(k, part, j).wait_send()
    for part in range(PARTS):
        for n in range(tiles):
            across(part, n).wait_send()
            keep(part, n).wait()
            for j in range(1, n_dp):
                out_copy(part, n, j).wait()


def fused(
    n_seq,
    n_dp,
    queries,
    new_keys,
    new_values,
    cache_keys,
    cache_values,
    keep_lengths,
    cache_doc,
    new_doc,
    out_weight,
):
    toks = queries.shape[1]
    slots = cache_keys.shape[1]
    cols = out_weight.shape[1]
    group = queries.shape[2] // cache_keys.shape[2]
    width = group * HD
    keys = slots + pl.cdiv(toks, LANES) * LANES
    tiles = 2
    part_toks = toks // PARTS
    dma = pltpu.SemaphoreType.DMA
    bf16 = jnp.bfloat16
    blocks = pl.pallas_call(
        functools.partial(fused_kernel, n_seq, n_dp, group),
        out_shape=jax.ShapeDtypeStruct((n_dp, toks, cols // 2), bf16),
        in_specs=[pl.BlockSpec(memory_space=pl.ANY)] * 5
        + [
            pl.BlockSpec(memory_space=pltpu.SMEM),
            pl.BlockSpec(memory_space=pltpu.VMEM),
            pl.BlockSpec(memory_space=pltpu.VMEM),
            pl.BlockSpec(memory_space=pl.ANY),
        ],
        out_specs=pl.BlockSpec(memory_space=pl.ANY),
        scratch_shapes=[
            pltpu.VMEM((n_seq, PARTS, part_toks, width), bf16),
            pltpu.VMEM((n_seq, keys, HD), bf16),
            pltpu.VMEM((n_seq, keys, HD), bf16),
            pltpu.VMEM((n_seq, 1, keys), jnp.float32),
            pltpu.VMEM((n_seq, PARTS, part_toks, width), bf16),
            pltpu.VMEM((n_seq, PARTS, n_dp, part_toks, width), bf16),
            pltpu.VMEM((n_seq, width, cols), bf16),
            pltpu.VMEM((PARTS, n_dp * part_toks, cols), jnp.float32),
            pltpu.VMEM((PARTS, tiles, n_dp * part_toks, cols // 2 // tiles), bf16),
            pltpu.VMEM((PARTS, tiles, n_dp * part_toks, cols // 2 // tiles), bf16),
            pltpu.VMEM((PARTS, tiles, n_dp, part_toks, cols // 2 // tiles), bf16),
            dma((5 + PARTS, n_seq)),
            dma((5 + PARTS, n_seq)),
            dma((n_seq, PARTS)),
            dma((n_seq, PARTS)),
            dma((n_seq, PARTS, n_dp)),
            dma((n_seq, PARTS, n_dp)),
            dma((PARTS, tiles)),
            dma((PARTS, tiles)),
            dma((PARTS, tiles, n_dp)),
            dma((PARTS, tiles, n_dp)),
            dma((n_seq,)),
        ],
        compiler_params=pltpu.CompilerParams(
            collective_id=0, has_side_effects=True, vmem_limit_bytes=56 << 20
        ),
    )(queries, new_keys, new_values, cache_keys, cache_values, keep_lengths, cache_doc, new_doc, out_weight)
    return blocks.transpose(1, 0, 2)[None]


def placed_local(mesh, *args):
    n_seq, n_dp, n_tensor = (mesh.shape[axis] for axis in ("seq", "dp", "tensor"))
    queries, cache_keys = args[0], args[3]
    local_kv = cache_keys.shape[2] // HD
    if local_kv == n_seq and n_tensor == 2 and queries.shape[1] <= LANES:
        return fused(n_seq, n_dp, *args)
    return local(*args)


def solution(mesh):
    placed = (
        P("dp", "seq", "tensor"),
        P("dp", "seq", "tensor"),
        P("dp", "seq", "tensor"),
        P("dp", "seq", "tensor"),
        P("dp", "seq", "tensor"),
        P("dp", "seq"),
        P("dp", "seq"),
        P("dp", "seq"),
        P("tensor", "dp"),
    )
    return jax.shard_map(
        functools.partial(placed_local, mesh),
        mesh=mesh,
        in_specs=placed,
        out_specs=P("dp", "seq", None, "tensor"),
        check_vma=False,
    )
```
